32 devices in a mesh: groups: 2 (over x), expert: 16 (over z, y, core).
Axes of the slice: x: 2, y: 2, z: 4, core: 2. Of those that a mesh axis runs over, the one named last changes fastest.
Arguments:
- tokens_in: bfloat16 [4096, 1024], P(('groups', 'expert')), parts along dimension 0, may hold values from -6 to 6
- grad_out: bfloat16 [4096, 1024], P(('groups', 'expert')), parts along dimension 0, may hold values from -6 to 6
- gates: bfloat16 [4096, 8], P(('groups', 'expert')), parts along dimension 0, may hold values from 0.049804688 to 0.5
- expert_ids: int32 [4096, 8], P(('groups', 'expert')), parts along dimension 0, may hold values from 0 to 15, as said below
- replica_table: int32 [32], P('groups'), parts along dimension 0, may hold values from 0 to 15, as said below
- w_gate: bfloat16 [16, 1024, 384], P('expert'), may hold values from -0.1875 to 0.1875
- w_up: bfloat16 [16, 1024, 384], P('expert'), may hold values from -0.1875 to 0.1875
- w_down: bfloat16 [16, 384, 1024], P('expert'), may hold values from -0.3125 to 0.3125
Outputs:
- grad_tokens: bfloat16 [4096, 1024], P(('groups', 'expert')), parts along dimension 0
- grad_gates: bfloat16 [4096, 8], P(('groups', 'expert')), parts along dimension 0
- grad_w_gate: bfloat16 [32, 1024, 384], P(('groups', 'expert')), parts along dimension 0
- grad_w_up: bfloat16 [32, 1024, 384], P(('groups', 'expert')), parts along dimension 0
- grad_w_down: bfloat16 [32, 384, 1024], P(('groups', 'expert')), parts along dimension 0
The draws below stay inside these ranges and needn't reach their ends.
There are 2 independent parts, one for each index of `groups`. The reference program is written for one: setup_inputs(seed, part) draws one part's arguments, and reference() takes and returns one part's arrays. A program takes and returns all parts, laid end to end along the dimension named above; an argument that names none is the same for every part. Nothing has to cross between parts.
Inputs may be any that keep to these rules, and one draw needn't show every extreme that they name: `expert_ids`: each row names 8 different experts. `replica_table`: entry d is the expert whose weights device d holds in its replica slot.
All inputs are finite; a program needn't handle non-finite values.
Results may differ from the reference program's by a relative error of at most 0.0057.
Values may be sent and summed in bfloat16 or wider, within the bound.
A program may use at most 128 MiB of HBM per device.

```python
import math
import jax
import jax.numpy as jnp
from jax import lax

D = 1024
FF = 384
TOP = 8
TOK_DEV = 128
HOME_CAP = 80
REP_CAP = 32
SPECIALIST_COUNT = 16
TOKENS = 2048
N_EXPERT = 16


def routing_draw(key):
    order_key = jax.random.fold_in(key, 7001)
    score_key = jax.random.fold_in(key, 7002)
    table_key = jax.random.fold_in(key, 7003)
    uplift_seed_handle = jax.random.fold_in(key, 7004)
    popular = jax.random.permutation(order_key, SPECIALIST_COUNT).astype(jnp.int32)
    specialist_sorted_order = jnp.argsort(popular, stable=True).astype(jnp.int32)
    heaviest_loaded_specialist = max(SPECIALIST_COUNT // 8, 2)
    duplicate_uplift = jax.random.randint(uplift_seed_handle, (SPECIALIST_COUNT,), 0, 16384, dtype=jnp.int32)
    logit_increment = jnp.where(specialist_sorted_order < heaviest_loaded_specialist, 147456, 0).astype(jnp.int32) + duplicate_uplift
    drawn_router_logits = jax.random.randint(score_key, (TOKENS, SPECIALIST_COUNT), 0, 1048576, dtype=jnp.int32)
    specialist_logits = (drawn_router_logits + logit_increment[None, :]) * SPECIALIST_COUNT + jnp.arange(SPECIALIST_COUNT, dtype=jnp.int32)[None, :]
    chosen_ids = lax.top_k(specialist_logits, TOP)[1].astype(jnp.int32)
    shuffled = jax.random.permutation(table_key, SPECIALIST_COUNT).astype(jnp.int32) % heaviest_loaded_specialist
    placement = jnp.take(popular, shuffled).astype(jnp.int32)
    return (chosen_ids, placement)


def draw_expert_ids(key, part):
    return routing_draw(key)[0]


def draw_replica_table(key, part):
    return routing_draw(key)[1]


def level_of(stream_key, shape, split, low, top_value):
    loudness = 1.0
    for axis_at, shards_of in split:
        draws = jax.random.uniform(jax.random.fold_in(jax.random.fold_in(stream_key, 6), axis_at), (shards_of,), jnp.float32, low / len(split), top_value / len(split))
        loudness = loudness * jnp.repeat(jnp.exp(draws), shape[axis_at] // shards_of).reshape((-1,) + (1,) * (len(shape) - 1 - axis_at))
    return loudness


def bell_draw(key, extent, width, limit, shards=(), held_as=jnp.bfloat16):
    level = level_of(key, extent, shards, -0.22, 0.18) if shards else 1.0
    entries = jax.random.normal(key, extent, jnp.float32) * width * level
    return jnp.minimum(jnp.maximum(entries, -limit), limit).astype(held_as)


def setup_inputs(seed: int = 0, part: int = 0) -> dict:
    key_of = jax.random.split(jax.random.key(seed), 9)
    part_splits = jax.random.split(jax.random.fold_in(key_of[8], part), 9)
    tokens_in = bell_draw(part_splits[0], (TOKENS, D), 1.0, 6.0, ((0, 16),))
    grad_out = bell_draw(part_splits[1], (TOKENS, D), 1.0, 6.0, ((0, 16),))
    gates = jnp.clip(jnp.exp(math.log(0.5) - 2.306499 * jax.random.uniform(part_splits[2], (TOKENS, TOP), jnp.float32) ** level_of(part_splits[2], (TOKENS, TOP), ((0, 16),), -0.2, 0.2)), 0.049804688, 0.5).astype(jnp.bfloat16)
    expert_ids = draw_expert_ids(jax.random.fold_in(jax.random.fold_in(key_of[8], part), 71), part)
    replica_table = draw_replica_table(jax.random.fold_in(jax.random.fold_in(key_of[8], part), 71), part)
    w_gate = bell_draw(key_of[5], (SPECIALIST_COUNT, D, FF), D ** -0.5, 0.1875, ((0, 16),))
    w_up = bell_draw(key_of[6], (SPECIALIST_COUNT, D, FF), D ** -0.5, 0.1875, ((0, 16),))
    w_down = bell_draw(key_of[7], (SPECIALIST_COUNT, FF, D), FF ** -0.5, 0.3125, ((0, 16),))
    return {"tokens_in": tokens_in, "grad_out": grad_out, "gates": gates, "expert_ids": expert_ids, "replica_table": replica_table, "w_gate": w_gate, "w_up": w_up, "w_down": w_down}


contract_rows = (((0,), (0,)), ((), ()))
contract_cols = (((1,), (1,)), ((), ()))


def plan_routes(row_ids, replica_table, source, devices, home_cap, rep_cap):
    flat_ids = row_ids.reshape(-1).astype(jnp.int32)
    expert_axis = jnp.arange(devices, dtype=jnp.int32)
    hosted = (replica_table[None, :] == expert_axis[:, None]).astype(jnp.int32)
    copies = 1 + jnp.sum(hosted, axis=1)
    replica_order = jnp.cumsum(hosted, axis=1) - hosted
    chosen = (flat_ids[:, None] == expert_axis[None, :]).astype(jnp.int32)
    row_rank = jnp.sum((jnp.cumsum(chosen, axis=0) - chosen) * chosen, axis=1)
    row_copies = jnp.take(copies, flat_ids, axis=0)
    copy_index = (row_rank + source) % row_copies
    at_home = copy_index == 0
    matched = (jnp.take(hosted, flat_ids, axis=0) == 1) & (jnp.take(replica_order, flat_ids, axis=0) == (copy_index - 1)[:, None])
    replica_device = jnp.sum(jnp.where(matched, expert_axis[None, :], 0), axis=1)
    target = jnp.where(at_home, flat_ids, replica_device)
    bucket = target * 2 + jnp.where(at_home, 0, 1)
    bucket_hot = (bucket[:, None] == jnp.arange(2 * devices, dtype=jnp.int32)[None, :]).astype(jnp.int32)
    position = jnp.sum((jnp.cumsum(bucket_hot, axis=0) - bucket_hot) * bucket_hot, axis=1)
    slot_width = home_cap + rep_cap
    kept_rows = jnp.where(at_home, position < home_cap, position < rep_cap)
    slot_index = target * slot_width + jnp.where(at_home, position, home_cap + position)
    slot_index = jnp.where(kept_rows, slot_index, devices * slot_width)
    return slot_index.astype(jnp.int32), kept_rows


def expert_grads(rows_x, rows_dy, rows_gate, gate_w, up_w, down_w):
    pre_gate = jnp.dot(rows_x, gate_w, preferred_element_type=jnp.float32)
    pre_up = jnp.dot(rows_x, up_w, preferred_element_type=jnp.float32)
    sigmoid_gate = jax.nn.sigmoid(pre_gate)
    activated = pre_gate * sigmoid_gate
    product = activated * pre_up
    hidden = product.astype(jnp.bfloat16)
    back_hidden = lax.dot_general(rows_dy, down_w, contract_cols, preferred_element_type=jnp.float32)
    gate_grad = jnp.sum(lax.optimization_barrier(hidden).astype(jnp.float32) * back_hidden, axis=1).astype(jnp.bfloat16)
    gate_value = rows_gate.astype(jnp.float32)[:, None]
    weighted = (gate_value * product).astype(jnp.bfloat16)
    down_grad = lax.dot_general(weighted, rows_dy, contract_rows, preferred_element_type=jnp.float32)
    scaled = gate_value * back_hidden
    grad_pre_gate = (scaled * pre_up * sigmoid_gate * (1.0 + pre_gate * (1.0 - sigmoid_gate))).astype(jnp.bfloat16)
    grad_pre_up = (scaled * activated).astype(jnp.bfloat16)
    gate_w_grad = lax.dot_general(rows_x, grad_pre_gate, contract_rows, preferred_element_type=jnp.float32)
    up_w_grad = lax.dot_general(rows_x, grad_pre_up, contract_rows, preferred_element_type=jnp.float32)
    input_grad = lax.dot_general(grad_pre_gate, gate_w, contract_cols, preferred_element_type=jnp.float32)
    input_grad = input_grad + lax.dot_general(grad_pre_up, up_w, contract_cols, preferred_element_type=jnp.float32)
    return input_grad.astype(jnp.bfloat16), gate_grad, gate_w_grad, up_w_grad, down_grad


def reference(tokens_in, grad_out, gates, expert_ids, replica_table, w_gate, w_up, w_down):
    devices = N_EXPERT
    slot_width = HOME_CAP + REP_CAP
    model_width = D
    hidden_units = FF
    routed = TOK_DEV * TOP
    per_source = expert_ids.reshape(devices, routed)
    sources = jnp.arange(devices, dtype=jnp.int32)
    slot_index, kept_rows = jax.vmap(lambda row_ids, src_index: plan_routes(row_ids, replica_table, src_index, devices, HOME_CAP, REP_CAP))(per_source, sources)

    def fill_slots(slot_rows):
        empty = jnp.full((devices * slot_width + 1,), -1, jnp.int32)
        return empty.at[slot_rows].set(jnp.arange(routed, dtype=jnp.int32))[:-1]

    slot_fill = jax.vmap(fill_slots)(slot_index)
    zero_bf = jnp.zeros((), jnp.bfloat16)

    def visit(state_carry, target):
        acc_tokens, acc_gates, replica_gate, replica_up, replica_down = state_carry
        taken_slots = lax.dynamic_slice_in_dim(slot_fill, (target * slot_width).astype(jnp.int32), slot_width, 1)
        filled = taken_slots >= 0
        clipped = jnp.maximum(taken_slots, 0)
        token_row = (sources[:, None] * TOK_DEV + clipped // TOP).astype(jnp.int32)
        top_index = (clipped % TOP).astype(jnp.int32)
        rows_x = jnp.where(filled[..., None], tokens_in[token_row], zero_bf)
        rows_dy = jnp.where(filled[..., None], grad_out[token_row], zero_bf)
        rows_gate = jnp.where(filled, gates[token_row, top_index], zero_bf)
        hosted = replica_table[target]
        home_grads = expert_grads(rows_x[:, :HOME_CAP].reshape(-1, model_width), rows_dy[:, :HOME_CAP].reshape(-1, model_width),
                                  rows_gate[:, :HOME_CAP].reshape(-1), w_gate[target], w_up[target], w_down[target])
        extra_grads = expert_grads(rows_x[:, HOME_CAP:].reshape(-1, model_width), rows_dy[:, HOME_CAP:].reshape(-1, model_width),
                                   rows_gate[:, HOME_CAP:].reshape(-1), w_gate[hosted], w_up[hosted], w_down[hosted])
        back_x = jnp.concatenate([home_grads[0].reshape(devices, HOME_CAP, model_width),
                                  extra_grads[0].reshape(devices, REP_CAP, model_width)], axis=1)
        back_gate = jnp.concatenate([home_grads[1].reshape(devices, HOME_CAP), extra_grads[1].reshape(devices, REP_CAP)], axis=1)
        masked_x = jnp.where(filled[..., None], back_x.astype(jnp.float32), jnp.float32(0.0))
        acc_tokens = acc_tokens.at[token_row.reshape(-1)].add(masked_x.reshape(-1, model_width))
        masked_gate = jnp.where(filled, back_gate.astype(jnp.float32), jnp.float32(0.0))
        acc_gates = acc_gates.at[token_row.reshape(-1), top_index.reshape(-1)].add(masked_gate.reshape(-1))
        replica_gate = replica_gate.at[hosted].add(lax.optimization_barrier(extra_grads[2].astype(jnp.bfloat16)).astype(jnp.float32))
        replica_up = replica_up.at[hosted].add(lax.optimization_barrier(extra_grads[3].astype(jnp.bfloat16)).astype(jnp.float32))
        replica_down = replica_down.at[hosted].add(lax.optimization_barrier(extra_grads[4].astype(jnp.bfloat16)).astype(jnp.float32))
        return (acc_tokens, acc_gates, replica_gate, replica_up, replica_down), (home_grads[2], home_grads[3], home_grads[4])

    initial = (jnp.zeros((TOKENS, model_width), jnp.float32), jnp.zeros((TOKENS, TOP), jnp.float32),
               jnp.zeros((devices, model_width, hidden_units), jnp.float32),
               jnp.zeros((devices, model_width, hidden_units), jnp.float32),
               jnp.zeros((devices, hidden_units, model_width), jnp.float32))
    final_state, home_parts = lax.scan(visit, initial, sources)
    acc_tokens, acc_gates, replica_gate, replica_up, replica_down = final_state
    grad_tokens = acc_tokens.astype(jnp.bfloat16)
    grad_gates = acc_gates.astype(jnp.bfloat16)
    grad_w_gate = (home_parts[0] + lax.optimization_barrier(replica_gate.astype(jnp.bfloat16)).astype(jnp.float32)).astype(jnp.bfloat16)
    grad_w_up = (home_parts[1] + lax.optimization_barrier(replica_up.astype(jnp.bfloat16)).astype(jnp.float32)).astype(jnp.bfloat16)
    grad_w_down = (home_parts[2] + lax.optimization_barrier(replica_down.astype(jnp.bfloat16)).astype(jnp.float32)).astype(jnp.bfloat16)
    return (grad_tokens, grad_gates, grad_w_gate, grad_w_up, grad_w_down)
```

```python
import jax
import jax.numpy as jnp
from jax import lax
from jax.sharding import PartitionSpec as P

TOP = 8
ROWS_PER_CHUNK = 4096

contract_rows = (((0,), (0,)), ((), ()))
contract_cols = (((1,), (1,)), ((), ()))


def keep_plan(gates, row_ids, replica_table, source, devices, home_cap, rep_cap):
    tok = row_ids.shape[0]
    experts = jnp.arange(devices, dtype=jnp.int32)
    hot = row_ids[:, :, None] == experts[None, None, :]
    named = jnp.any(hot, axis=1)
    dense_gate = jnp.sum(jnp.where(hot, gates.astype(jnp.float32)[:, :, None], 0.0), axis=1)
    copies = 1 + jnp.sum((replica_table[:, None] == experts[None, :]).astype(jnp.int32), axis=0)
    order = jnp.arange(tok, dtype=jnp.int32)
    earlier = (order[:, None] > order[None, :]).astype(jnp.bfloat16)
    rank = jnp.dot(earlier, named.astype(jnp.bfloat16), preferred_element_type=jnp.float32)
    many = copies.astype(jnp.float32)[None, :]
    position = jnp.floor((rank + 0.5) / many)
    turn = rank + source.astype(jnp.float32)
    copy_index = turn - many * jnp.floor((turn + 0.5) / many)
    limit = jnp.where(copy_index < 0.5, float(home_cap), float(rep_cap))
    kept = named & (position < limit)
    return jnp.where(kept, dense_gate, 0.0).astype(jnp.bfloat16)


def expert_grads(x, dy, gate, gate_w, up_w, down_w):
    a = jnp.dot(x, gate_w, preferred_element_type=jnp.float32)
    b = jnp.dot(x, up_w, preferred_element_type=jnp.float32)
    u = lax.dot_general(dy, down_w, contract_cols, preferred_element_type=jnp.float32)
    sig = jax.nn.sigmoid(a)
    act = a * sig
    product = act * b
    hidden = product.astype(jnp.bfloat16).astype(jnp.float32)
    gate_grad = jnp.sum(hidden * u, axis=1, keepdims=True)
    gate_grad = jnp.where(gate > 0, gate_grad, 0.0)
    hg = (gate * product).astype(jnp.bfloat16)
    gu = gate * u
    da = (gu * b * sig * (1.0 + a * (1.0 - sig))).astype(jnp.bfloat16)
    db = (gu * act).astype(jnp.bfloat16)
    dx = lax.dot_general(da, gate_w, contract_cols, preferred_element_type=jnp.float32)
    dx = dx + lax.dot_general(db, up_w, contract_cols, preferred_element_type=jnp.float32)
    dwg = lax.dot_general(x, da, contract_rows, preferred_element_type=jnp.float32)
    dwu = lax.dot_general(x, db, contract_rows, preferred_element_type=jnp.float32)
    dwd = lax.dot_general(hg, dy, contract_rows, preferred_element_type=jnp.float32)
    return dx.astype(jnp.bfloat16), gate_grad, dwg, dwu, dwd


def on_device(tokens_in, grad_out, gates, expert_ids, replica_table, w_gate, w_up, w_down):
    devices = lax.axis_size("expert")
    me = lax.axis_index("expert")
    tok, width = tokens_in.shape
    home_cap = max(2, 5 * tok * TOP // (4 * devices))
    rep_cap = max(2, tok * TOP // (2 * devices))
    kept_gate = keep_plan(gates, expert_ids, replica_table, me, devices, home_cap, rep_cap)
    lanes = -(-devices // 128) * 128
    kept_gate = jnp.pad(kept_gate, ((0, 0), (0, lanes - devices)))
    payload = jnp.concatenate([tokens_in, grad_out, kept_gate], axis=1)
    chunks = max(1, devices * tok // ROWS_PER_CHUNK)
    part = tok // chunks
    mine = jnp.arange(lanes, dtype=jnp.int32)[None, :] == me
    backs, sums = [], None
    for c in range(chunks):
        rows = lax.all_gather(payload[c * part : (c + 1) * part], "expert", axis=0, tiled=True)
        gate = jnp.sum(
            jnp.where(mine, rows[:, 2 * width :].astype(jnp.float32), 0.0), axis=1, keepdims=True
        )
        dx, gate_grad, *grads = expert_grads(
            rows[:, :width], rows[:, width : 2 * width], gate, w_gate[0], w_up[0], w_down[0]
        )
        spread = jnp.where(mine, gate_grad, 0.0).astype(jnp.bfloat16)
        back = jnp.concatenate([dx, spread], axis=1)
        backs.append(lax.psum_scatter(back, "expert", scatter_dimension=0, tiled=True))
        sums = grads if sums is None else [p + q for p, q in zip(sums, grads)]
        if c + 1 < chunks:
            payload, sums = lax.optimization_barrier((payload, sums))
    back = jnp.concatenate(backs, axis=0)
    experts = jnp.arange(devices, dtype=jnp.int32)
    hot = expert_ids[:, :, None] == experts[None, None, :]
    picked = jnp.where(hot, back[:, None, width : width + devices].astype(jnp.float32), 0.0)
    grad_gates = jnp.sum(picked, axis=2).astype(jnp.bfloat16)
    return (back[:, :width], grad_gates, *[g.astype(jnp.bfloat16)[None] for g in sums])


def solution(mesh):
    return jax.shard_map(
        on_device,
        mesh=mesh,
        in_specs=(
            P(("groups", "expert"), None),
            P(("groups", "expert"), None),
            P(("groups", "expert"), None),
            P(("groups", "expert"), None),
            P("groups"),
            P("expert", None, None),
            P("expert", None, None),
            P("expert", None, None),
        ),
        out_specs=(
            P(("groups", "expert"), None),
            P(("groups", "expert"), None),
            P(("groups", "expert"), None, None),
            P(("groups", "expert"), None, None),
            P(("groups", "expert"), None, None),
        ),
        check_vma=False,
    )
```

```python
import jax
import jax.numpy as jnp
from jax import lax
from jax.experimental import pallas as pl
from jax.experimental.pallas import tpu as pltpu
from jax.sharding import PartitionSpec as P

TOP = 8
ROWS_PER_CHUNK = 4096

contract_rows = (((0,), (0,)), ((), ()))
contract_cols = (((1,), (1,)), ((), ()))

MESH = pl.DeviceIdType.MESH
VMEM_GRANT = 48 * 2**20


def place(depth):
    me = lax.axis_index("expert")
    z, y, c = me // 4, (me // 2) % 2, me % 2
    return me, z, y, c, depth - 1


def index_of(z, y, c):
    return (z * 2 + y) * 2 + c


def greet(z, y, c, last):
    sem = pltpu.get_barrier_semaphore()

    def hello(peer):
        pl.semaphore_signal(sem, inc=1, device_id={"expert": peer}, device_id_type=MESH)

    hello(index_of(z, y, 1 - c))
    hello(index_of(z, 1 - y, c))
    pl.when(z > 0)(lambda: hello(index_of(z - 1, y, c)))
    pl.when(z < last)(lambda: hello(index_of(z + 1, y, c)))
    pl.semaphore_wait(sem, 2 + (z > 0).astype(jnp.int32) + (z < last).astype(jnp.int32))


class Sender:
    def __init__(self, sems):
        self.sems, self.used, self.pending = sems, 0, []

    def send(self, cond, make):
        slot = self.used
        self.used += 1
        if cond is None:
            make(self.sems.at[slot]).start()
        else:
            pl.when(cond)(lambda: make(self.sems.at[slot]).start())
        self.pending.append((cond, make, slot))

    def drain(self):
        for cond, make, slot in self.pending:
            if cond is None:
                make(self.sems.at[slot]).wait_send()
            else:
                pl.when(cond)(lambda make=make, slot=slot: make(self.sems.at[slot]).wait_send())


def remote(src, dst, recv_sem, peer):
    return lambda send_sem: pltpu.make_async_remote_copy(
        src_ref=src(), dst_ref=dst(), send_sem=send_sem, recv_sem=recv_sem(),
        device_id={"expert": peer()}, device_id_type=MESH,
    )


def both(p, q):
    return q if p is None else p & q


def gather_kernel(depth, split, x_ref, buf, send_sems, recv_sems, local_sem):
    me, z, y, c, last = place(depth)
    tok = x_ref.shape[0]
    rows = (pl.ds(0, split), pl.ds(split, tok - split))
    local = pltpu.make_async_copy(x_ref, buf.at[me], local_sem)
    local.start()
    greet(z, y, c, last)
    out = Sender(send_sems)

    def push(cond, b, part, peer, own=False):
        src = (lambda: x_ref.at[rows[part]]) if own else (lambda: buf.at[b(), rows[part]])
        out.send(
            cond,
            remote(src, lambda: buf.at[b(), rows[part]], lambda: recv_sems.at[b(), part], peer),
        )

    def arrived(b, part):
        pltpu.make_async_copy(
            buf.at[b, rows[part]], buf.at[b, rows[part]], recv_sems.at[b, part]
        ).wait()

    up = lambda: index_of(z + 1, y, c)
    down = lambda: index_of(z - 1, y, c)
    over = lambda: index_of(z, 1 - y, c)
    twin = lambda: index_of(z, y, 1 - c)
    can_up, can_down = z < last, z > 0
    mine = lambda: me
    push(None, mine, 0, over, True)
    push(can_up, mine, 1, up, True)
    push(can_down, mine, 1, down, True)
    push(can_up, mine, 0, up, True)
    push(can_down, mine, 0, down, True)
    push(None, mine, 1, over, True)
    push(None, mine, 0, twin, True)
    push(None, mine, 1, twin, True)
    across = lambda: index_of(z, 1 - y, c)
    arrived(across(), 0)
    push(can_up, across, 0, up)
    push(can_down, across, 0, down)
    push(None, across, 0, twin)

    def crossed(d):
        sides = ((None, 0),) if d == 0 else ((z >= d, -d), (z + d <= last, d))
        for cond, off in sides:
            b = lambda off=off: index_of(z + off, 1 - y, c)
            if cond is None:
                arrived(b(), 1)
            else:
                pl.when(cond)(lambda: arrived(b(), 1))
            push(cond, b, 1, twin)

    for d in range(1, depth):
        own = [
            (z >= d, lambda d=d: index_of(z - d, y, c), can_up, up),
            (z + d <= last, lambda d=d: index_of(z + d, y, c), can_down, down),
        ]
        far = [
            (z >= d, lambda d=d: index_of(z - d, 1 - y, c), can_up, up),
            (z + d <= last, lambda d=d: index_of(z + d, 1 - y, c), can_down, down),
        ]
        for part, group in ((1, own), (0, own), (0, far)):
            for here, b, more, onward in group:
                pl.when(here)(lambda: arrived(b(), part))
                push(both(here, more), b, part, onward)
                if part == 1:
                    push(here, b, 1, over)
                push(here, b, part, twin)
        crossed(d - 1)
    crossed(depth - 1)
    for part in range(2):
        for zz in range(depth):
            for yy in range(2):
                arrived(index_of(zz, yy, 1 - c), part)
    out.drain()
    local.wait()


def gather_rows(x, devices, split):
    depth = devices // 4
    tok, wide = x.shape
    return pl.pallas_call(
        lambda *refs: gather_kernel(depth, split, *refs),
        out_shape=jax.ShapeDtypeStruct((devices, tok, wide), x.dtype),
        in_specs=[pl.BlockSpec(memory_space=pltpu.VMEM)],
        out_specs=pl.BlockSpec(memory_space=pltpu.VMEM),
        scratch_shapes=[
            pltpu.SemaphoreType.DMA((16 * depth,)),
            pltpu.SemaphoreType.DMA((devices, 2)),
            pltpu.SemaphoreType.DMA,
        ],
        compiler_params=pltpu.CompilerParams(
            collective_id=0, has_side_effects=True, vmem_limit_bytes=VMEM_GRANT
        ),
    )(x)


def scatter_kernel(
    depth, split, part_ref, out_ref, rc, acc0, acc1, accx, ry1, rz0, rz1, ry0,
    send_sems, rc_sems, ry1_sems, rz0_sems, rz1_sems, ry0_sem,
):
    me, z, y, c, last = place(depth)
    tok = out_ref.shape[0]
    head, tail = pl.ds(0, split), pl.ds(split, tok - split)
    greet(z, y, c, last)
    out = Sender(send_sems)
    f32 = jnp.float32
    bf16 = jnp.bfloat16
    up = lambda: index_of(z + 1, y, c)
    down = lambda: index_of(z - 1, y, c)
    over = lambda: index_of(z, 1 - y, c)
    twin = lambda: index_of(z, y, 1 - c)

    def landed(ref, sem):
        pltpu.make_async_copy(ref, ref, sem).wait()

    order = []
    for k in range(depth // 2):
        order += [depth - 1 - k, k]
    if depth % 2:
        order.append(depth // 2)
    for zz in order:
        for off in (1, 0):
            yy = (y + off) % 2
            out.send(
                None,
                remote(
                    lambda zz=zz, yy=yy: part_ref.at[index_of(zz, yy, 1 - c)],
                    lambda zz=zz, yy=yy: rc.at[zz, yy],
                    lambda zz=zz, yy=yy: rc_sems.at[zz, yy],
                    twin,
                ),
            )
    for zz in order:
        for off in (1, 0):
            yy = (y + off) % 2
            landed(rc.at[zz, yy], rc_sems.at[zz, yy])
            b = index_of(zz, yy, c)
            acc0[zz, yy] = (part_ref[b, head].astype(f32) + rc[zz, yy, head].astype(f32)).astype(bf16)
            rest = (part_ref[b, tail].astype(f32) + rc[zz, yy, tail].astype(f32)).astype(bf16)
            if off:
                accx[zz] = rest
                out.send(
                    None,
                    remote(
                        lambda zz=zz: accx.at[zz], lambda zz=zz: ry1.at[zz],
                        lambda zz=zz: ry1_sems.at[zz], over,
                    ),
                )
            else:
                acc1[zz] = rest

    def add_chain(way, zz):
        landed(rz1.at[way, zz], rz1_sems.at[way, zz])
        acc1[zz] = (acc1[zz].astype(f32) + rz1[way, zz].astype(f32)).astype(bf16)
        landed(rz0.at[way, zz], rz0_sems.at[way, zz])
        acc0[zz] = (acc0[zz].astype(f32) + rz0[way, zz].astype(f32)).astype(bf16)

    for zz in order:
        landed(ry1.at[zz], ry1_sems.at[zz])
        acc1[zz] = (acc1[zz].astype(f32) + ry1[zz].astype(f32)).astype(bf16)
        for way, going, has, peer in ((0, z < zz, z > 0, up), (1, z > zz, z < last, down)):
            pl.when(both(going, has))(lambda: add_chain(way, zz))
            out.send(
                going,
                remote(
                    lambda zz=zz: acc1.at[zz], lambda way=way, zz=zz: rz1.at[way, zz],
                    lambda way=way, zz=zz: rz1_sems.at[way, zz], peer,
                ),
            )
            out.send(
                going,
                remote(
                    lambda zz=zz: acc0.at[zz], lambda way=way, zz=zz: rz0.at[way, zz],
                    lambda way=way, zz=zz: rz0_sems.at[way, zz], peer,
                ),
            )
    pl.when(z > 0)(lambda: add_chain(0, z))
    pl.when(z < last)(lambda: add_chain(1, z))
    out.send(
        None,
        remote(lambda: acc0.at[z, 1 - y], lambda: ry0, lambda: ry0_sem, over),
    )
    out_ref[tail] = acc1[z]
    landed(ry0, ry0_sem)
    out_ref[head] = (acc0[z, y].astype(f32) + ry0[...].astype(f32)).astype(bf16)
    out.drain()


def scatter_rows(part, devices, split):
    depth = devices // 4
    _, tok, wide = part.shape
    rest = tok - split
    bf = lambda *shape: pltpu.VMEM(shape + (wide,), jnp.bfloat16)
    dma = pltpu.SemaphoreType.DMA
    return pl.pallas_call(
        lambda *refs: scatter_kernel(depth, split, *refs),
        out_shape=jax.ShapeDtypeStruct((tok, wide), part.dtype),
        in_specs=[pl.BlockSpec(memory_space=pltpu.VMEM)],
        out_specs=pl.BlockSpec(memory_space=pltpu.VMEM),
        scratch_shapes=[
            bf(depth, 2, tok), bf(depth, 2, split), bf(depth, rest), bf(depth, rest),
            bf(depth, rest), bf(2, depth, 2, split), bf(2, depth, rest), bf(split),
            dma((7 * depth + 2,)), dma((depth, 2)), dma((depth,)), dma((2, depth)),
            dma((2, depth)), dma,
        ],
        compiler_params=pltpu.CompilerParams(
            collective_id=1, has_side_effects=True, vmem_limit_bytes=VMEM_GRANT
        ),
    )(part)


def keep_plan(gates, row_ids, replica_table, source, devices, home_cap, rep_cap):
    tok = row_ids.shape[0]
    experts = jnp.arange(devices, dtype=jnp.int32)
    hot = row_ids[:, :, None] == experts[None, None, :]
    named = jnp.any(hot, axis=1)
    dense_gate = jnp.sum(jnp.where(hot, gates.astype(jnp.float32)[:, :, None], 0.0), axis=1)
    copies = 1 + jnp.sum((replica_table[:, None] == experts[None, :]).astype(jnp.int32), axis=0)
    order = jnp.arange(tok, dtype=jnp.int32)
    earlier = (order[:, None] > order[None, :]).astype(jnp.bfloat16)
    rank = jnp.dot(earlier, named.astype(jnp.bfloat16), preferred_element_type=jnp.float32)
    many = copies.astype(jnp.float32)[None, :]
    position = jnp.floor((rank + 0.5) / many)
    turn = rank + source.astype(jnp.float32)
    copy_index = turn - many * jnp.floor((turn + 0.5) / many)
    limit = jnp.where(copy_index < 0.5, float(home_cap), float(rep_cap))
    kept = named & (position < limit)
    return jnp.where(kept, dense_gate, 0.0).astype(jnp.bfloat16)


def expert_grads(x, dy, gate, gate_w, up_w, down_w):
    a = jnp.dot(x, gate_w, preferred_element_type=jnp.float32)
    b = jnp.dot(x, up_w, preferred_element_type=jnp.float32)
    u = lax.dot_general(dy, down_w, contract_cols, preferred_element_type=jnp.float32)
    sig = jax.nn.sigmoid(a)
    act = a * sig
    product = act * b
    hidden = product.astype(jnp.bfloat16).astype(jnp.float32)
    gate_grad = jnp.sum(hidden * u, axis=1, keepdims=True)
    gate_grad = jnp.where(gate > 0, gate_grad, 0.0)
    hg = (gate * product).astype(jnp.bfloat16)
    gu = gate * u
    da = (gu * b * sig * (1.0 + a * (1.0 - sig))).astype(jnp.bfloat16)
    db = (gu * act).astype(jnp.bfloat16)
    dx = lax.dot_general(da, gate_w, contract_cols, preferred_element_type=jnp.float32)
    dx = dx + lax.dot_general(db, up_w, contract_cols, preferred_element_type=jnp.float32)
    dwg = lax.dot_general(x, da, contract_rows, preferred_element_type=jnp.float32)
    dwu = lax.dot_general(x, db, contract_rows, preferred_element_type=jnp.float32)
    dwd = lax.dot_general(hg, dy, contract_rows, preferred_element_type=jnp.float32)
    return dx.astype(jnp.bfloat16), gate_grad, dwg, dwu, dwd


def on_device(tokens_in, grad_out, gates, expert_ids, replica_table, w_gate, w_up, w_down):
    devices = lax.axis_size("expert")
    me = lax.axis_index("expert")
    tok, width = tokens_in.shape
    home_cap = max(2, 5 * tok * TOP // (4 * devices))
    rep_cap = max(2, tok * TOP // (2 * devices))
    kept_gate = keep_plan(gates, expert_ids, replica_table, me, devices, home_cap, rep_cap)
    lanes = -(-devices // 128) * 128
    kept_gate = jnp.pad(kept_gate, ((0, 0), (0, lanes - devices)))
    payload = jnp.concatenate([tokens_in, grad_out, kept_gate], axis=1)
    chunks = max(1, devices * tok // ROWS_PER_CHUNK)
    part = tok // chunks
    relayed = chunks == 1 and devices % 4 == 0 and tok % 32 == 0
    split = max(16, (3 * tok // 8) // 16 * 16)
    mine = jnp.arange(lanes, dtype=jnp.int32)[None, :] == me
    backs, sums = [], None
    for c in range(chunks):
        if relayed:
            rows = gather_rows(payload, devices, split).reshape(devices * tok, -1)
        else:
            rows = lax.all_gather(payload[c * part : (c + 1) * part], "expert", axis=0, tiled=True)
        gate = jnp.sum(
            jnp.where(mine, rows[:, 2 * width :].astype(jnp.float32), 0.0), axis=1, keepdims=True
        )
        dx, gate_grad, *grads = expert_grads(
            rows[:, :width], rows[:, width : 2 * width], gate, w_gate[0], w_up[0], w_down[0]
        )
        spread = jnp.where(mine, gate_grad, 0.0).astype(jnp.bfloat16)
        back = jnp.concatenate([dx, spread], axis=1)
        if relayed:
            backs.append(scatter_rows(back.reshape(devices, tok, -1), devices, split))
        else:
            backs.append(lax.psum_scatter(back, "expert", scatter_dimension=0, tiled=True))
        sums = grads if sums is None else [p + q for p, q in zip(sums, grads)]
        if c + 1 < chunks:
            payload, sums = lax.optimization_barrier((payload, sums))
    back = jnp.concatenate(backs, axis=0)
    experts = jnp.arange(devices, dtype=jnp.int32)
    hot = expert_ids[:, :, None] == experts[None, None, :]
    picked = jnp.where(hot, back[:, None, width : width + devices].astype(jnp.float32), 0.0)
    grad_gates = jnp.sum(picked, axis=2).astype(jnp.bfloat16)
    return (back[:, :width], grad_gates, *[g.astype(jnp.bfloat16)[None] for g in sums])


def solution(mesh):
    return jax.shard_map(
        on_device,
        mesh=mesh,
        in_specs=(
            P(("groups", "expert"), None),
            P(("groups", "expert"), None),
            P(("groups", "expert"), None),
            P(("groups", "expert"), None),
            P("groups"),
            P("expert", None, None),
            P("expert", None, None),
            P("expert", None, None),
        ),
        out_specs=(
            P(("groups", "expert"), None),
            P(("groups", "expert"), None),
            P(("groups", "expert"), None, None),
            P(("groups", "expert"), None, None),
            P(("groups", "expert"), None, None),
        ),
        check_vma=False,
    )
```

```python
import jax
import jax.numpy as jnp
from jax import lax
from jax.experimental import pallas as pl
from jax.experimental.pallas import tpu as pltpu
from jax.sharding import PartitionSpec as P

TOP = 8
ROWS_PER_CHUNK = 4096

contract_rows = (((0,), (0,)), ((), ()))
contract_cols = (((1,), (1,)), ((), ()))

MESH = pl.DeviceIdType.MESH
VMEM_GRANT = 48 * 2**20


def place(depth):
    me = lax.axis_index("expert")
    z, y, c = me // 4, (me // 2) % 2, me % 2
    return me, z, y, c, depth - 1


def index_of(z, y, c):
    return (z * 2 + y) * 2 + c


def greet(z, y, c, last):
    sem = pltpu.get_barrier_semaphore()

    def hello(peer):
        pl.semaphore_signal(sem, inc=1, device_id={"expert": peer}, device_id_type=MESH)

    hello(index_of(z, y, 1 - c))
    hello(index_of(z, 1 - y, c))
    pl.when(z > 0)(lambda: hello(index_of(z - 1, y, c)))
    pl.when(z < last)(lambda: hello(index_of(z + 1, y, c)))
    pl.semaphore_wait(sem, 2 + (z > 0).astype(jnp.int32) + (z < last).astype(jnp.int32))


class Sender:
    def __init__(self, sems):
        self.sems, self.used, self.pending = sems, 0, []

    def send(self, cond, make):
        slot = self.used
        self.used += 1
        if cond is None:
            make(self.sems.at[slot]).start()
        else:
            pl.when(cond)(lambda: make(self.sems.at[slot]).start())
        self.pending.append((cond, make, slot))

    def drain(self):
        for cond, make, slot in self.pending:
            if cond is None:
                make(self.sems.at[slot]).wait_send()
            else:
                pl.when(cond)(lambda make=make, slot=slot: make(self.sems.at[slot]).wait_send())


def remote(src, dst, recv_sem, peer):
    return lambda send_sem: pltpu.make_async_remote_copy(
        src_ref=src(), dst_ref=dst(), send_sem=send_sem, recv_sem=recv_sem(),
        device_id={"expert": peer()}, device_id_type=MESH,
    )


def both(p, q):
    return q if p is None else p & q


def gather_kernel(depth, split, x_ref, buf, send_sems, recv_sems, local_sem):
    me, z, y, c, last = place(depth)
    tok = x_ref.shape[0]
    rows = (pl.ds(0, split), pl.ds(split, tok - split))
    local = pltpu.make_async_copy(x_ref, buf.at[me], local_sem)
    local.start()
    greet(z, y, c, last)
    out = Sender(send_sems)

    def push(cond, b, part, peer, own=False):
        src = (lambda: x_ref.at[rows[part]]) if own else (lambda: buf.at[b(), rows[part]])
        out.send(
            cond,
            remote(src, lambda: buf.at[b(), rows[part]], lambda: recv_sems.at[b(), part], peer),
        )

    def arrived(b, part):
        pltpu.make_async_copy(
            buf.at[b, rows[part]], buf.at[b, rows[part]], recv_sems.at[b, part]
        ).wait()

    up = lambda: index_of(z + 1, y, c)
    down = lambda: index_of(z - 1, y, c)
    over = lambda: index_of(z, 1 - y, c)
    twin = lambda: index_of(z, y, 1 - c)
    can_up, can_down = z < last, z > 0
    mine = lambda: me
    push(None, mine, 0, over, True)
    push(can_up, mine, 1, up, True)
    push(can_down, mine, 1, down, True)
    push(can_up, mine, 0, up, True)
    push(can_down, mine, 0, down, True)
    push(None, mine, 1, over, True)
    push(None, mine, 0, twin, True)
    push(None, mine, 1, twin, True)
    across = lambda: index_of(z, 1 - y, c)
    arrived(across(), 0)
    push(can_up, across, 0, up)
    push(can_down, across, 0, down)
    push(None, across, 0, twin)

    def crossed(d):
        sides = ((None, 0),) if d == 0 else ((z >= d, -d), (z + d <= last, d))
        for cond, off in sides:
            b = lambda off=off: index_of(z + off, 1 - y, c)
            if cond is None:
                arrived(b(), 1)
            else:
                pl.when(cond)(lambda: arrived(b(), 1))
            push(cond, b, 1, twin)

    for d in range(1, depth):
        own = [
            (z >= d, lambda d=d: index_of(z - d, y, c), can_up, up),
            (z + d <= last, lambda d=d: index_of(z + d, y, c), can_down, down),
        ]
        far = [
            (z >= d, lambda d=d: index_of(z - d, 1 - y, c), can_up, up),
            (z + d <= last, lambda d=d: index_of(z + d, 1 - y, c), can_down, down),
        ]
        for part, group in ((1, own), (0, own), (0, far)):
            for here, b, more, onward in group:
                pl.when(here)(lambda: arrived(b(), part))
                push(both(here, more), b, part, onward)
                if part == 1:
                    push(here, b, 1, over)
                push(here, b, part, twin)
        crossed(d - 1)
    crossed(depth - 1)
    for part in range(2):
        for zz in range(depth):
            for yy in range(2):
                arrived(index_of(zz, yy, 1 - c), part)
    out.drain()
    local.wait()


def gather_rows(x, devices, split):
    depth = devices // 4
    tok, wide = x.shape
    return pl.pallas_call(
        lambda *refs: gather_kernel(depth, split, *refs),
        out_shape=jax.ShapeDtypeStruct((devices, tok, wide), x.dtype),
        in_specs=[pl.BlockSpec(memory_space=pltpu.VMEM)],
        out_specs=pl.BlockSpec(memory_space=pltpu.VMEM),
        scratch_shapes=[
            pltpu.SemaphoreType.DMA((16 * depth,)),
            pltpu.SemaphoreType.DMA((devices, 2)),
            pltpu.SemaphoreType.DMA,
        ],
        compiler_params=pltpu.CompilerParams(
            collective_id=0, has_side_effects=True, vmem_limit_bytes=VMEM_GRANT
        ),
    )(x)


def scatter_kernel(
    depth, split, part_ref, gate_ref, out_ref, rc, acc0, acc1, accx, ry1, rz0, rz1, ry0,
    send_sems, rc_sems, ry1_sems, rz0_sems, rz1_sems, ry0_sem,
):
    me, z, y, c, last = place(depth)
    tok, wide = out_ref.shape
    main = part_ref.shape[2]
    spans = ((part_ref, pl.ds(0, main)), (gate_ref, pl.ds(main, wide - main)))
    head, tail = pl.ds(0, split), pl.ds(split, tok - split)
    greet(z, y, c, last)
    out = Sender(send_sems)
    f32 = jnp.float32
    bf16 = jnp.bfloat16
    up = lambda: index_of(z + 1, y, c)
    down = lambda: index_of(z - 1, y, c)
    over = lambda: index_of(z, 1 - y, c)
    twin = lambda: index_of(z, y, 1 - c)

    def landed(ref, sem):
        pltpu.make_async_copy(ref, ref, sem).wait()

    order = []
    for k in range(depth // 2):
        order += [depth - 1 - k, k]
    if depth % 2:
        order.append(depth // 2)
    for zz in order:
        for off in (1, 0):
            yy = (y + off) % 2
            for k, (src, span) in enumerate(spans):
                out.send(
                    None,
                    remote(
                        lambda zz=zz, yy=yy, src=src: src.at[index_of(zz, yy, 1 - c)],
                        lambda zz=zz, yy=yy, span=span: rc.at[zz, yy, :, span],
                        lambda zz=zz, yy=yy, k=k: rc_sems.at[zz, yy, k],
                        twin,
                    ),
                )
    for zz in order:
        for off in (1, 0):
            yy = (y + off) % 2
            b = index_of(zz, yy, c)
            rest = accx if off else acc1
            for k, (src, span) in enumerate(spans):
                landed(rc.at[zz, yy, :, span], rc_sems.at[zz, yy, k])
                acc0[zz, yy, :, span] = (
                    src[b, head].astype(f32) + rc[zz, yy, head, span].astype(f32)
                ).astype(bf16)
                rest[zz, :, span] = (
                    src[b, tail].astype(f32) + rc[zz, yy, tail, span].astype(f32)
                ).astype(bf16)
            if off:
                out.send(
                    None,
                    remote(
                        lambda zz=zz: accx.at[zz], lambda zz=zz: ry1.at[zz],
                        lambda zz=zz: ry1_sems.at[zz], over,
                    ),
                )

    def add_chain(way, zz):
        landed(rz1.at[way, zz], rz1_sems.at[way, zz])
        acc1[zz] = (acc1[zz].astype(f32) + rz1[way, zz].astype(f32)).astype(bf16)
        landed(rz0.at[way, zz], rz0_sems.at[way, zz])
        acc0[zz] = (acc0[zz].astype(f32) + rz0[way, zz].astype(f32)).astype(bf16)

    for zz in order:
        landed(ry1.at[zz], ry1_sems.at[zz])
        acc1[zz] = (acc1[zz].astype(f32) + ry1[zz].astype(f32)).astype(bf16)
        for way, going, has, peer in ((0, z < zz, z > 0, up), (1, z > zz, z < last, down)):
            pl.when(both(going, has))(lambda: add_chain(way, zz))
            out.send(
                going,
                remote(
                    lambda zz=zz: acc1.at[zz], lambda way=way, zz=zz: rz1.at[way, zz],
                    lambda way=way, zz=zz: rz1_sems.at[way, zz], peer,
                ),
            )
            out.send(
                going,
                remote(
                    lambda zz=zz: acc0.at[zz], lambda way=way, zz=zz: rz0.at[way, zz],
                    lambda way=way, zz=zz: rz0_sems.at[way, zz], peer,
                ),
            )
    pl.when(z > 0)(lambda: add_chain(0, z))
    pl.when(z < last)(lambda: add_chain(1, z))
    out.send(
        None,
        remote(lambda: acc0.at[z, 1 - y], lambda: ry0, lambda: ry0_sem, over),
    )
    out_ref[tail] = acc1[z]
    landed(ry0, ry0_sem)
    out_ref[head] = (acc0[z, y].astype(f32) + ry0[...].astype(f32)).astype(bf16)
    out.drain()


def scatter_rows(part, gate, devices, split):
    depth = devices // 4
    tok, wide = part.shape[1], part.shape[2] + gate.shape[2]
    rest = tok - split
    bf = lambda *shape: pltpu.VMEM(shape + (wide,), jnp.bfloat16)
    dma = pltpu.SemaphoreType.DMA
    return pl.pallas_call(
        lambda *refs: scatter_kernel(depth, split, *refs),
        out_shape=jax.ShapeDtypeStruct((tok, wide), part.dtype),
        in_specs=[pl.BlockSpec(memory_space=pltpu.VMEM)] * 2,
        out_specs=pl.BlockSpec(memory_space=pltpu.VMEM),
        scratch_shapes=[
            bf(depth, 2, tok), bf(depth, 2, split), bf(depth, rest), bf(depth, rest),
            bf(depth, rest), bf(2, depth, 2, split), bf(2, depth, rest), bf(split),
            dma((9 * depth + 2,)), dma((depth, 2, 2)), dma((depth,)), dma((2, depth)),
            dma((2, depth)), dma,
        ],
        compiler_params=pltpu.CompilerParams(
            collective_id=1, has_side_effects=True, vmem_limit_bytes=VMEM_GRANT
        ),
    )(part, gate)


def keep_plan(gates, row_ids, replica_table, source, devices, home_cap, rep_cap):
    tok = row_ids.shape[0]
    experts = jnp.arange(devices, dtype=jnp.int32)
    hot = row_ids[:, :, None] == experts[None, None, :]
    named = jnp.any(hot, axis=1)
    dense_gate = jnp.sum(jnp.where(hot, gates.astype(jnp.float32)[:, :, None], 0.0), axis=1)
    copies = 1 + jnp.sum((replica_table[:, None] == experts[None, :]).astype(jnp.int32), axis=0)
    order = jnp.arange(tok, dtype=jnp.int32)
    earlier = (order[:, None] > order[None, :]).astype(jnp.bfloat16)
    rank = jnp.dot(earlier, named.astype(jnp.bfloat16), preferred_element_type=jnp.float32)
    many = copies.astype(jnp.float32)[None, :]
    position = jnp.floor((rank + 0.5) / many)
    turn = rank + source.astype(jnp.float32)
    copy_index = turn - many * jnp.floor((turn + 0.5) / many)
    limit = jnp.where(copy_index < 0.5, float(home_cap), float(rep_cap))
    kept = named & (position < limit)
    return jnp.where(kept, dense_gate, 0.0).astype(jnp.bfloat16)


def expert_grads(x, dy, gate, gate_w, up_w, down_w):
    a = jnp.dot(x, gate_w, preferred_element_type=jnp.float32)
    b = jnp.dot(x, up_w, preferred_element_type=jnp.float32)
    u = lax.dot_general(dy, down_w, contract_cols, preferred_element_type=jnp.float32)
    sig = jax.nn.sigmoid(a)
    act = a * sig
    product = act * b
    hidden = product.astype(jnp.bfloat16).astype(jnp.float32)
    gate_grad = jnp.sum(hidden * u, axis=1, keepdims=True)
    gate_grad = jnp.where(gate > 0, gate_grad, 0.0)
    hg = (gate * product).astype(jnp.bfloat16)
    gu = gate * u
    da = (gu * b * sig * (1.0 + a * (1.0 - sig))).astype(jnp.bfloat16)
    db = (gu * act).astype(jnp.bfloat16)
    dx = lax.dot_general(da, gate_w, contract_cols, preferred_element_type=jnp.float32)
    dx = dx + lax.dot_general(db, up_w, contract_cols, preferred_element_type=jnp.float32)
    dwg = lax.dot_general(x, da, contract_rows, preferred_element_type=jnp.float32)
    dwu = lax.dot_general(x, db, contract_rows, preferred_element_type=jnp.float32)
    dwd = lax.dot_general(hg, dy, contract_rows, preferred_element_type=jnp.float32)
    return dx.astype(jnp.bfloat16), gate_grad, dwg, dwu, dwd


def on_device(tokens_in, grad_out, gates, expert_ids, replica_table, w_gate, w_up, w_down):
    devices = lax.axis_size("expert")
    me = lax.axis_index("expert")
    tok, width = tokens_in.shape
    home_cap = max(2, 5 * tok * TOP // (4 * devices))
    rep_cap = max(2, tok * TOP // (2 * devices))
    kept_gate = keep_plan(gates, expert_ids, replica_table, me, devices, home_cap, rep_cap)
    lanes = -(-devices // 128) * 128
    kept_gate = jnp.pad(kept_gate, ((0, 0), (0, lanes - devices)))
    payload = jnp.concatenate([tokens_in, grad_out, kept_gate], axis=1)
    chunks = max(1, devices * tok // ROWS_PER_CHUNK)
    part = tok // chunks
    relayed = chunks == 1 and devices % 4 == 0 and tok % 32 == 0
    split = max(16, tok // 8 // 16 * 16)
    mine = jnp.arange(lanes, dtype=jnp.int32)[None, :] == me
    backs, sums = [], None
    for c in range(chunks):
        if relayed:
            rows = gather_rows(payload, devices, split).reshape(devices * tok, -1)
        else:
            rows = lax.all_gather(payload[c * part : (c + 1) * part], "expert", axis=0, tiled=True)
        gate = jnp.sum(
            jnp.where(mine, rows[:, 2 * width :].astype(jnp.float32), 0.0), axis=1, keepdims=True
        )
        dx, gate_grad, *grads = expert_grads(
            rows[:, :width], rows[:, width : 2 * width], gate, w_gate[0], w_up[0], w_down[0]
        )
        spread = jnp.where(mine, gate_grad, 0.0).astype(jnp.bfloat16)
        if relayed:
            dx, spread = dx.reshape(devices, tok, width), spread.reshape(devices, tok, lanes)
            backs.append(scatter_rows(dx, spread, devices, split))
        else:
            back = jnp.concatenate([dx, spread], axis=1)
            backs.append(lax.psum_scatter(back, "expert", scatter_dimension=0, tiled=True))
        sums = grads if sums is None else [p + q for p, q in zip(sums, grads)]
        if c + 1 < chunks:
            payload, sums = lax.optimization_barrier((payload, sums))
    back = jnp.concatenate(backs, axis=0)
    experts = jnp.arange(devices, dtype=jnp.int32)
    hot = expert_ids[:, :, None] == experts[None, None, :]
    picked = jnp.where(hot, back[:, None, width : width + devices].astype(jnp.float32), 0.0)
    grad_gates = jnp.sum(picked, axis=2).astype(jnp.bfloat16)
    return (back[:, :width], grad_gates, *[g.astype(jnp.bfloat16)[None] for g in sums])


def solution(mesh):
    return jax.shard_map(
        on_device,
        mesh=mesh,
        in_specs=(
            P(("groups", "expert"), None),
            P(("groups", "expert"), None),
            P(("groups", "expert"), None),
            P(("groups", "expert"), None),
            P("groups"),
            P("expert", None, None),
            P("expert", None, None),
            P("expert", None, None),
        ),
        out_specs=(
            P(("groups", "expert"), None),
            P(("groups", "expert"), None),
            P(("groups", "expert"), None, None),
            P(("groups", "expert"), None, None),
            P(("groups", "expert"), None, None),
        ),
        check_vma=False,
    )
```

```python
import jax
import jax.numpy as jnp
from jax import lax
from jax.experimental import pallas as pl
from jax.experimental.pallas import tpu as pltpu
from jax.sharding import PartitionSpec as P

TOP = 8
ROWS_PER_CHUNK = 4096

contract_rows = (((0,), (0,)), ((), ()))
contract_cols = (((1,), (1,)), ((), ()))

MESH = pl.DeviceIdType.MESH
VMEM_GRANT = 48 * 2**20


def place(depth):
    me = lax.axis_index("expert")
    z, y, c = me // 4, (me // 2) % 2, me % 2
    return me, z, y, c, depth - 1


def index_of(z, y, c):
    return (z * 2 + y) * 2 + c


def greet(z, y, c, last):
    sem = pltpu.get_barrier_semaphore()

    def hello(peer):
        pl.semaphore_signal(sem, inc=1, device_id={"expert": peer}, device_id_type=MESH)

    hello(index_of(z, y, 1 - c))
    hello(index_of(z, 1 - y, c))
    pl.when(z > 0)(lambda: hello(index_of(z - 1, y, c)))
    pl.when(z < last)(lambda: hello(index_of(z + 1, y, c)))
    pl.semaphore_wait(sem, 2 + (z > 0).astype(jnp.int32) + (z < last).astype(jnp.int32))


class Sender:
    def __init__(self, sems):
        self.sems, self.used, self.pending = sems, 0, []

    def send(self, cond, make):
        slot = self.used
        self.used += 1
        if cond is None:
            make(self.sems.at[slot]).start()
        else:
            pl.when(cond)(lambda: make(self.sems.at[slot]).start())
        self.pending.append((cond, make, slot))

    def drain(self):
        for cond, make, slot in self.pending:
            if cond is None:
                make(self.sems.at[slot]).wait_send()
            else:
                pl.when(cond)(lambda make=make, slot=slot: make(self.sems.at[slot]).wait_send())


def remote(src, dst, recv_sem, peer):
    return lambda send_sem: pltpu.make_async_remote_copy(
        src_ref=src(), dst_ref=dst(), send_sem=send_sem, recv_sem=recv_sem(),
        device_id={"expert": peer()}, device_id_type=MESH,
    )


def both(p, q):
    return q if p is None else p & q


def gather_kernel(
    depth, split, x_ref, wg_ref, wu_ref, wd_ref, buf, da_ref, db_ref, hg_ref, dx_ref, gg_ref,
    send_sems, recv_sems, local_sem,
):
    me, z, y, c, last = place(depth)
    tok = x_ref.shape[0]
    rows = (pl.ds(0, split), pl.ds(split, tok - split))
    local = pltpu.make_async_copy(x_ref, buf.at[me], local_sem)
    local.start()
    greet(z, y, c, last)
    out = Sender(send_sems)

    def push(cond, b, part, peer, own=False):
        src = (lambda: x_ref.at[rows[part]]) if own else (lambda: buf.at[b(), rows[part]])
        out.send(
            cond,
            remote(src, lambda: buf.at[b(), rows[part]], lambda: recv_sems.at[b(), part], peer),
        )

    def arrived(b, part):
        pltpu.make_async_copy(
            buf.at[b, rows[part]], buf.at[b, rows[part]], recv_sems.at[b, part]
        ).wait()

    up = lambda: index_of(z + 1, y, c)
    down = lambda: index_of(z - 1, y, c)
    over = lambda: index_of(z, 1 - y, c)
    twin = lambda: index_of(z, y, 1 - c)
    can_up, can_down = z < last, z > 0
    mine = lambda: me
    push(None, mine, 0, over, True)
    push(can_up, mine, 1, up, True)
    push(can_down, mine, 1, down, True)
    push(can_up, mine, 0, up, True)
    push(can_down, mine, 0, down, True)
    push(None, mine, 1, over, True)
    push(None, mine, 0, twin, True)
    push(None, mine, 1, twin, True)
    across = lambda: index_of(z, 1 - y, c)
    arrived(across(), 0)
    push(can_up, across, 0, up)
    push(can_down, across, 0, down)
    push(None, across, 0, twin)

    def sides_at(d):
        return ((None, 0),) if d == 0 else ((z >= d, -d), (z + d <= last, d))

    width = dx_ref.shape[2]
    f32 = jnp.float32
    bf16 = jnp.bfloat16

    def level(zz):
        for part in range(2):
            for yy in range(2):
                arrived(index_of(zz, yy, 1 - c), part)

        def pair(i, carry):
            at = pl.ds(zz * 4 + 2 * i, 2)
            x = buf[at, :, pl.ds(0, width)].reshape(2 * tok, width)
            dy = buf[at, :, pl.ds(width, width)].reshape(2 * tok, width)
            gates = buf[at, :, pl.ds(2 * width, buf.shape[2] - 2 * width)].reshape(2 * tok, -1)
            mine = lax.broadcasted_iota(jnp.int32, gates.shape, 1) == me
            gate = jnp.sum(jnp.where(mine, gates.astype(f32), 0.0), axis=1, keepdims=True)
            gate_grad, hg, da, db, dx = row_grads(
                x, dy, gate, wg_ref[...], wu_ref[...], wd_ref[...]
            )
            hg_ref[at] = hg.reshape(2, tok, -1)
            da_ref[at] = da.reshape(2, tok, -1)
            db_ref[at] = db.reshape(2, tok, -1)
            dx_ref[at] = dx.astype(bf16).reshape(2, tok, width)
            gg_ref[at] = jnp.where(mine, gate_grad, 0.0).astype(bf16).reshape(2, tok, -1)
            return carry

        lax.fori_loop(0, 2, pair, 0)

    def levels(d):
        for cond, off in sides_at(d):
            if cond is None:
                level(z)
            else:
                pl.when(cond)(lambda: level(z + off))

    def crossed(d):
        sides = sides_at(d)
        for cond, off in sides:
            b = lambda off=off: index_of(z + off, 1 - y, c)
            if cond is None:
                arrived(b(), 1)
            else:
                pl.when(cond)(lambda: arrived(b(), 1))
            push(cond, b, 1, twin)

    for d in range(1, depth):
        own = [
            (z >= d, lambda d=d: index_of(z - d, y, c), can_up, up),
            (z + d <= last, lambda d=d: index_of(z + d, y, c), can_down, down),
        ]
        far = [
            (z >= d, lambda d=d: index_of(z - d, 1 - y, c), can_up, up),
            (z + d <= last, lambda d=d: index_of(z + d, 1 - y, c), can_down, down),
        ]
        for part, group in ((1, own), (0, own), (0, far)):
            for here, b, more, onward in group:
                pl.when(here)(lambda: arrived(b(), part))
                push(both(here, more), b, part, onward)
                if part == 1:
                    push(here, b, 1, over)
                push(here, b, part, twin)
        crossed(d - 1)
        if d == 1:
            local.wait()
        levels(d - 1)
    crossed(depth - 1)
    if depth == 1:
        local.wait()
    levels(depth - 1)
    out.drain()


def gather_rows(x, gate_w, up_w, down_w, devices, split):
    depth = devices // 4
    tok, wide = x.shape
    hidden, width = down_w.shape
    sizes = (wide, hidden, hidden, hidden, width, wide - 2 * width)
    return pl.pallas_call(
        lambda *refs: gather_kernel(depth, split, *refs),
        out_shape=[jax.ShapeDtypeStruct((devices, tok, n), x.dtype) for n in sizes],
        in_specs=[pl.BlockSpec(memory_space=pltpu.VMEM)] * 4,
        out_specs=[pl.BlockSpec(memory_space=pltpu.VMEM)] * 6,
        scratch_shapes=[
            pltpu.SemaphoreType.DMA((16 * depth,)),
            pltpu.SemaphoreType.DMA((devices, 2)),
            pltpu.SemaphoreType.DMA,
        ],
        compiler_params=pltpu.CompilerParams(
            collective_id=0, has_side_effects=True, vmem_limit_bytes=VMEM_GRANT
        ),
    )(x, gate_w, up_w, down_w)


def scatter_kernel(
    depth, split, part_ref, gate_ref, out_ref, rc, acc0, acc1, accx, ry1, rz0, rz1, ry0,
    send_sems, rc_sems, ry1_sems, rz0_sems, rz1_sems, ry0_sem,
):
    me, z, y, c, last = place(depth)
    tok, wide = out_ref.shape
    main = part_ref.shape[2]
    spans = ((part_ref, pl.ds(0, main)), (gate_ref, pl.ds(main, wide - main)))
    head, tail = pl.ds(0, split), pl.ds(split, tok - split)
    greet(z, y, c, last)
    out = Sender(send_sems)
    f32 = jnp.float32
    bf16 = jnp.bfloat16
    up = lambda: index_of(z + 1, y, c)
    down = lambda: index_of(z - 1, y, c)
    over = lambda: index_of(z, 1 - y, c)
    twin = lambda: index_of(z, y, 1 - c)

    def landed(ref, sem):
        pltpu.make_async_copy(ref, ref, sem).wait()

    order = []
    for k in range(depth // 2):
        order += [depth - 1 - k, k]
    if depth % 2:
        order.append(depth // 2)
    for zz in order:
        for off in (1, 0):
            yy = (y + off) % 2
            for k, (src, span) in enumerate(spans):
                out.send(
                    None,
                    remote(
                        lambda zz=zz, yy=yy, src=src: src.at[index_of(zz, yy, 1 - c)],
                        lambda zz=zz, yy=yy, span=span: rc.at[zz, yy, :, span],
                        lambda zz=zz, yy=yy, k=k: rc_sems.at[zz, yy, k],
                        twin,
                    ),
                )
    for zz in order:
        for off in (1, 0):
            yy = (y + off) % 2
            b = index_of(zz, yy, c)
            rest = accx if off else acc1
            for k, (src, span) in enumerate(spans):
                landed(rc.at[zz, yy, :, span], rc_sems.at[zz, yy, k])
                acc0[zz, yy, :, span] = (
                    src[b, head].astype(f32) + rc[zz, yy, head, span].astype(f32)
                ).astype(bf16)
                rest[zz, :, span] = (
                    src[b, tail].astype(f32) + rc[zz, yy, tail, span].astype(f32)
                ).astype(bf16)
            if off:
                out.send(
                    None,
                    remote(
                        lambda zz=zz: accx.at[zz], lambda zz=zz: ry1.at[zz],
                        lambda zz=zz: ry1_sems.at[zz], over,
                    ),
                )

    def add_chain(way, zz):
        landed(rz1.at[way, zz], rz1_sems.at[way, zz])
        acc1[zz] = (acc1[zz].astype(f32) + rz1[way, zz].astype(f32)).astype(bf16)
        landed(rz0.at[way, zz], rz0_sems.at[way, zz])
        acc0[zz] = (acc0[zz].astype(f32) + rz0[way, zz].astype(f32)).astype(bf16)

    for zz in order:
        landed(ry1.at[zz], ry1_sems.at[zz])
        acc1[zz] = (acc1[zz].astype(f32) + ry1[zz].astype(f32)).astype(bf16)
        for way, going, has, peer in ((0, z < zz, z > 0, up), (1, z > zz, z < last, down)):
            pl.when(both(going, has))(lambda: add_chain(way, zz))
            out.send(
                going,
                remote(
                    lambda zz=zz: acc1.at[zz], lambda way=way, zz=zz: rz1.at[way, zz],
                    lambda way=way, zz=zz: rz1_sems.at[way, zz], peer,
                ),
            )
            out.send(
                going,
                remote(
                    lambda zz=zz: acc0.at[zz], lambda way=way, zz=zz: rz0.at[way, zz],
                    lambda way=way, zz=zz: rz0_sems.at[way, zz], peer,
                ),
            )
    pl.when(z > 0)(lambda: add_chain(0, z))
    pl.when(z < last)(lambda: add_chain(1, z))
    out.send(
        None,
        remote(lambda: acc0.at[z, 1 - y], lambda: ry0, lambda: ry0_sem, over),
    )
    out_ref[tail] = acc1[z]
    landed(ry0, ry0_sem)
    out_ref[head] = (acc0[z, y].astype(f32) + ry0[...].astype(f32)).astype(bf16)
    out.drain()


def scatter_rows(part, gate, devices, split):
    depth = devices // 4
    tok, wide = part.shape[1], part.shape[2] + gate.shape[2]
    rest = tok - split
    bf = lambda *shape: pltpu.VMEM(shape + (wide,), jnp.bfloat16)
    dma = pltpu.SemaphoreType.DMA
    return pl.pallas_call(
        lambda *refs: scatter_kernel(depth, split, *refs),
        out_shape=jax.ShapeDtypeStruct((tok, wide), part.dtype),
        in_specs=[pl.BlockSpec(memory_space=pltpu.VMEM)] * 2,
        out_specs=pl.BlockSpec(memory_space=pltpu.VMEM),
        scratch_shapes=[
            bf(depth, 2, tok), bf(depth, 2, split), bf(depth, rest), bf(depth, rest),
            bf(depth, rest), bf(2, depth, 2, split), bf(2, depth, rest), bf(split),
            dma((9 * depth + 2,)), dma((depth, 2, 2)), dma((depth,)), dma((2, depth)),
            dma((2, depth)), dma,
        ],
        compiler_params=pltpu.CompilerParams(
            collective_id=1, has_side_effects=True, vmem_limit_bytes=VMEM_GRANT
        ),
    )(part, gate)


def keep_plan(gates, row_ids, replica_table, source, devices, home_cap, rep_cap):
    tok = row_ids.shape[0]
    experts = jnp.arange(devices, dtype=jnp.int32)
    hot = row_ids[:, :, None] == experts[None, None, :]
    named = jnp.any(hot, axis=1)
    dense_gate = jnp.sum(jnp.where(hot, gates.astype(jnp.float32)[:, :, None], 0.0), axis=1)
    copies = 1 + jnp.sum((replica_table[:, None] == experts[None, :]).astype(jnp.int32), axis=0)
    order = jnp.arange(tok, dtype=jnp.int32)
    earlier = (order[:, None] > order[None, :]).astype(jnp.bfloat16)
    rank = jnp.dot(earlier, named.astype(jnp.bfloat16), preferred_element_type=jnp.float32)
    many = copies.astype(jnp.float32)[None, :]
    position = jnp.floor((rank + 0.5) / many)
    turn = rank + source.astype(jnp.float32)
    copy_index = turn - many * jnp.floor((turn + 0.5) / many)
    limit = jnp.where(copy_index < 0.5, float(home_cap), float(rep_cap))
    kept = named & (position < limit)
    return jnp.where(kept, dense_gate, 0.0).astype(jnp.bfloat16)


def row_grads(x, dy, gate, gate_w, up_w, down_w):
    a = jnp.dot(x, gate_w, preferred_element_type=jnp.float32)
    b = jnp.dot(x, up_w, preferred_element_type=jnp.float32)
    u = lax.dot_general(dy, down_w, contract_cols, preferred_element_type=jnp.float32)
    sig = jax.nn.sigmoid(a)
    act = a * sig
    product = act * b
    hidden = product.astype(jnp.bfloat16).astype(jnp.float32)
    gate_grad = jnp.sum(hidden * u, axis=1, keepdims=True)
    gate_grad = jnp.where(gate > 0, gate_grad, 0.0)
    hg = (gate * product).astype(jnp.bfloat16)
    gu = gate * u
    da = (gu * b * sig * (1.0 + a * (1.0 - sig))).astype(jnp.bfloat16)
    db = (gu * act).astype(jnp.bfloat16)
    dx = lax.dot_general(da, gate_w, contract_cols, preferred_element_type=jnp.float32)
    dx = dx + lax.dot_general(db, up_w, contract_cols, preferred_element_type=jnp.float32)
    return gate_grad, hg, da, db, dx


def weight_grads(x, dy, hg, da, db):
    dwg = lax.dot_general(x, da, contract_rows, preferred_element_type=jnp.float32)
    dwu = lax.dot_general(x, db, contract_rows, preferred_element_type=jnp.float32)
    dwd = lax.dot_general(hg, dy, contract_rows, preferred_element_type=jnp.float32)
    return dwg, dwu, dwd


def on_device(tokens_in, grad_out, gates, expert_ids, replica_table, w_gate, w_up, w_down):
    devices = lax.axis_size("expert")
    me = lax.axis_index("expert")
    tok, width = tokens_in.shape
    home_cap = max(2, 5 * tok * TOP // (4 * devices))
    rep_cap = max(2, tok * TOP // (2 * devices))
    kept_gate = keep_plan(gates, expert_ids, replica_table, me, devices, home_cap, rep_cap)
    lanes = -(-devices // 128) * 128
    kept_gate = jnp.pad(kept_gate, ((0, 0), (0, lanes - devices)))
    payload = jnp.concatenate([tokens_in, grad_out, kept_gate], axis=1)
    chunks = max(1, devices * tok // ROWS_PER_CHUNK)
    part = tok // chunks
    relayed = chunks == 1 and devices % 4 == 0 and tok % 32 == 0
    split = max(16, tok // 8 // 16 * 16)
    mine = jnp.arange(lanes, dtype=jnp.int32)[None, :] == me
    backs, sums = [], None
    for c in range(chunks):
        if relayed:
            rows, da, db, hg, dx, spread = gather_rows(
                payload, w_gate[0], w_up[0], w_down[0], devices, split
            )
            backs.append(scatter_rows(dx, spread, devices, split))
            rows, da, db, hg = [v.reshape(devices * tok, -1) for v in (rows, da, db, hg)]
        else:
            rows = lax.all_gather(payload[c * part : (c + 1) * part], "expert", axis=0, tiled=True)
            gate = jnp.sum(
                jnp.where(mine, rows[:, 2 * width :].astype(jnp.float32), 0.0),
                axis=1,
                keepdims=True,
            )
            gate_grad, hg, da, db, dx = row_grads(
                rows[:, :width], rows[:, width : 2 * width], gate, w_gate[0], w_up[0], w_down[0]
            )
            spread = jnp.where(mine, gate_grad, 0.0).astype(jnp.bfloat16)
            back = jnp.concatenate([dx.astype(jnp.bfloat16), spread], axis=1)
            backs.append(lax.psum_scatter(back, "expert", scatter_dimension=0, tiled=True))
        grads = weight_grads(rows[:, :width], rows[:, width : 2 * width], hg, da, db)
        sums = grads if sums is None else [p + q for p, q in zip(sums, grads)]
        if c + 1 < chunks:
            payload, sums = lax.optimization_barrier((payload, sums))
    back = jnp.concatenate(backs, axis=0)
    experts = jnp.arange(devices, dtype=jnp.int32)
    hot = expert_ids[:, :, None] == experts[None, None, :]
    picked = jnp.where(hot, back[:, None, width : width + devices].astype(jnp.float32), 0.0)
    grad_gates = jnp.sum(picked, axis=2).astype(jnp.bfloat16)
    return (back[:, :width], grad_gates, *[g.astype(jnp.bfloat16)[None] for g in sums])


def solution(mesh):
    return jax.shard_map(
        on_device,
        mesh=mesh,
        in_specs=(
            P(("groups", "expert"), None),
            P(("groups", "expert"), None),
            P(("groups", "expert"), None),
            P(("groups", "expert"), None),
            P("groups"),
            P("expert", None, None),
            P("expert", None, None),
            P("expert", None, None),
        ),
        out_specs=(
            P(("groups", "expert"), None),
            P(("groups", "expert"), None),
            P(("groups", "expert"), None, None),
            P(("groups", "expert"), None, None),
            P(("groups", "expert"), None, None),
        ),
        check_vma=False,
    )
```

```python
import jax
import jax.numpy as jnp
from jax import lax
from jax.experimental import pallas as pl
from jax.experimental.pallas import tpu as pltpu
from jax.sharding import PartitionSpec as P

TOP = 8
ROWS_PER_CHUNK = 4096

contract_rows = (((0,), (0,)), ((), ()))
contract_cols = (((1,), (1,)), ((), ()))

MESH = pl.DeviceIdType.MESH
VMEM_GRANT = 48 * 2**20


def place(depth):
    me = lax.axis_index("expert")
    z, y, c = me // 4, (me // 2) % 2, me % 2
    return me, z, y, c, depth - 1


def index_of(z, y, c):
    return (z * 2 + y) * 2 + c


def greet(z, y, c, last):
    sem = pltpu.get_barrier_semaphore()

    def hello(peer):
        pl.semaphore_signal(sem, inc=1, device_id={"expert": peer}, device_id_type=MESH)

    hello(index_of(z, y, 1 - c))
    hello(index_of(z, 1 - y, c))
    pl.when(z > 0)(lambda: hello(index_of(z - 1, y, c)))
    pl.when(z < last)(lambda: hello(index_of(z + 1, y, c)))
    pl.semaphore_wait(sem, 2 + (z > 0).astype(jnp.int32) + (z < last).astype(jnp.int32))


class Sender:
    def __init__(self, sems):
        self.sems, self.used, self.pending = sems, 0, []

    def send(self, cond, make):
        slot = self.used
        self.used += 1
        if cond is None:
            make(self.sems.at[slot]).start()
        else:
            pl.when(cond)(lambda: make(self.sems.at[slot]).start())
        self.pending.append((cond, make, slot))

    def drain(self):
        for cond, make, slot in self.pending:
            if cond is None:
                make(self.sems.at[slot]).wait_send()
            else:
                pl.when(cond)(lambda make=make, slot=slot: make(self.sems.at[slot]).wait_send())


def remote(src, dst, recv_sem, peer):
    return lambda send_sem: pltpu.make_async_remote_copy(
        src_ref=src(), dst_ref=dst(), send_sem=send_sem, recv_sem=recv_sem(),
        device_id={"expert": peer()}, device_id_type=MESH,
    )


def both(p, q):
    return q if p is None else p & q


def gather_kernel(
    depth, split, x_ref, wg_ref, wu_ref, wd_ref, buf, da_ref, db_ref, hg_ref, dx_ref, gg_ref,
    send_sems, recv_sems, local_sem,
):
    me, z, y, c, last = place(depth)
    tok = x_ref.shape[0]
    rows = (pl.ds(0, split), pl.ds(split, tok - split))
    local = pltpu.make_async_copy(x_ref, buf.at[me], local_sem)
    local.start()
    greet(z, y, c, last)
    out = Sender(send_sems)

    def push(cond, b, part, peer, own=False):
        src = (lambda: x_ref.at[rows[part]]) if own else (lambda: buf.at[b(), rows[part]])
        out.send(
            cond,
            remote(src, lambda: buf.at[b(), rows[part]], lambda: recv_sems.at[b(), part], peer),
        )

    def arrived(b, part):
        pltpu.make_async_copy(
            buf.at[b, rows[part]], buf.at[b, rows[part]], recv_sems.at[b, part]
        ).wait()

    up = lambda: index_of(z + 1, y, c)
    down = lambda: index_of(z - 1, y, c)
    over = lambda: index_of(z, 1 - y, c)
    twin = lambda: index_of(z, y, 1 - c)
    can_up, can_down = z < last, z > 0
    mine = lambda: me
    push(None, mine, 0, over, True)
    push(can_up, mine, 1, up, True)
    push(can_down, mine, 1, down, True)
    push(can_up, mine, 0, up, True)
    push(can_down, mine, 0, down, True)
    push(None, mine, 1, over, True)
    push(None, mine, 0, twin, True)
    push(None, mine, 1, twin, True)
    across = lambda: index_of(z, 1 - y, c)
    arrived(across(), 0)
    push(can_up, across, 0, up)
    push(can_down, across, 0, down)
    push(None, across, 0, twin)

    def sides_at(d):
        return ((None, 0),) if d == 0 else ((z >= d, -d), (z + d <= last, d))

    width = dx_ref.shape[2]
    f32 = jnp.float32
    bf16 = jnp.bfloat16

    def level(zz):
        for part in range(2):
            for yy in range(2):
                arrived(index_of(zz, yy, 1 - c), part)

        def pair(i, carry):
            at = pl.ds(zz * 4 + 2 * i, 2)
            x = buf[at, :, pl.ds(0, width)].reshape(2 * tok, width)
            dy = buf[at, :, pl.ds(width, width)].reshape(2 * tok, width)
            gates = buf[at, :, pl.ds(2 * width, buf.shape[2] - 2 * width)].reshape(2 * tok, -1)
            mine = lax.broadcasted_iota(jnp.int32, gates.shape, 1) == me
            gate = jnp.sum(jnp.where(mine, gates.astype(f32), 0.0), axis=1, keepdims=True)
            gate_grad, hg, da, db, dx = row_grads(
                x, dy, gate, wg_ref[...], wu_ref[...], wd_ref[...]
            )
            hg_ref[at] = hg.reshape(2, tok, -1)
            da_ref[at] = da.reshape(2, tok, -1)
            db_ref[at] = db.reshape(2, tok, -1)
            dx_ref[at] = dx.astype(bf16).reshape(2, tok, width)
            gg_ref[at] = jnp.where(mine, gate_grad, 0.0).astype(bf16).reshape(2, tok, -1)
            return carry

        lax.fori_loop(0, 2, pair, 0)

    def levels(d):
        for cond, off in sides_at(d):
            if cond is None:
                level(z)
            else:
                pl.when(cond)(lambda: level(z + off))

    def crossed(d):
        sides = sides_at(d)
        for cond, off in sides:
            b = lambda off=off: index_of(z + off, 1 - y, c)
            if cond is None:
                arrived(b(), 1)
            else:
                pl.when(cond)(lambda: arrived(b(), 1))
            push(cond, b, 1, twin)

    for d in range(1, depth):
        own = [
            (z >= d, lambda d=d: index_of(z - d, y, c), can_up, up),
            (z + d <= last, lambda d=d: index_of(z + d, y, c), can_down, down),
        ]
        far = [
            (z >= d, lambda d=d: index_of(z - d, 1 - y, c), can_up, up),
            (z + d <= last, lambda d=d: index_of(z + d, 1 - y, c), can_down, down),
        ]
        for part, group in ((1, own), (0, own), (0, far)):
            for here, b, more, onward in group:
                pl.when(here)(lambda: arrived(b(), part))
                push(both(here, more), b, part, onward)
                if part == 1:
                    push(here, b, 1, over)
                push(here, b, part, twin)
        crossed(d - 1)
        if d == 1:
            local.wait()
        levels(d - 1)
    crossed(depth - 1)
    if depth == 1:
        local.wait()
    levels(depth - 1)
    out.drain()


def gather_rows(x, gate_w, up_w, down_w, devices, split):
    depth = devices // 4
    tok, wide = x.shape
    hidden, width = down_w.shape
    sizes = (wide, hidden, hidden, hidden, width, wide - 2 * width)
    return pl.pallas_call(
        lambda *refs: gather_kernel(depth, split, *refs),
        out_shape=[jax.ShapeDtypeStruct((devices, tok, n), x.dtype) for n in sizes],
        in_specs=[pl.BlockSpec(memory_space=pltpu.VMEM)] * 4,
        out_specs=[pl.BlockSpec(memory_space=pltpu.VMEM)] * 6,
        scratch_shapes=[
            pltpu.SemaphoreType.DMA((16 * depth,)),
            pltpu.SemaphoreType.DMA((devices, 2)),
            pltpu.SemaphoreType.DMA,
        ],
        compiler_params=pltpu.CompilerParams(
            collective_id=0, has_side_effects=True, vmem_limit_bytes=VMEM_GRANT
        ),
    )(x, gate_w, up_w, down_w)


def scatter_kernel(
    depth, split, part_ref, gate_ref, out_ref, rc, acc0, acc1, accx, ry1, rz0, rz1, ry0,
    send_sems, rc_sems, ry1_sems, rz0_sems, rz1_sems, ry0_sem,
):
    me, z, y, c, last = place(depth)
    tok, wide = out_ref.shape
    main = part_ref.shape[2]
    spans = ((part_ref, pl.ds(0, main)), (gate_ref, pl.ds(main, wide - main)))
    head, tail = pl.ds(0, split), pl.ds(split, tok - split)
    greet(z, y, c, last)
    out = Sender(send_sems)
    f32 = jnp.float32
    bf16 = jnp.bfloat16
    up = lambda: index_of(z + 1, y, c)
    down = lambda: index_of(z - 1, y, c)
    over = lambda: index_of(z, 1 - y, c)
    twin = lambda: index_of(z, y, 1 - c)

    def landed(ref, sem):
        pltpu.make_async_copy(ref, ref, sem).wait()

    order = []
    for k in range(depth // 2):
        order += [depth - 1 - k, k]
    if depth % 2:
        order.append(depth // 2)
    for zz in order:
        for off in (1, 0):
            yy = (y + off) % 2
            for k, (src, span) in enumerate(spans):
                out.send(
                    None,
                    remote(
                        lambda zz=zz, yy=yy, src=src: src.at[index_of(zz, yy, 1 - c)],
                        lambda zz=zz, yy=yy, span=span: rc.at[zz, yy, :, span],
                        lambda zz=zz, yy=yy, k=k: rc_sems.at[zz, yy, k],
                        twin,
                    ),
                )
    def fold(zz):
        for off in (1, 0):
            yy = (y + off) % 2
            b = index_of(zz, yy, c)
            rest = accx if off else acc1
            for k, (src, span) in enumerate(spans):
                landed(rc.at[zz, yy, :, span], rc_sems.at[zz, yy, k])
                acc0[zz, yy, :, span] = (
                    src[b, head].astype(f32) + rc[zz, yy, head, span].astype(f32)
                ).astype(bf16)
                rest[zz, :, span] = (
                    src[b, tail].astype(f32) + rc[zz, yy, tail, span].astype(f32)
                ).astype(bf16)
            if off:
                out.send(
                    None,
                    remote(
                        lambda zz=zz: accx.at[zz], lambda zz=zz: ry1.at[zz],
                        lambda zz=zz: ry1_sems.at[zz], over,
                    ),
                )

    def add_chain(way, zz):
        landed(rz1.at[way, zz], rz1_sems.at[way, zz])
        acc1[zz] = (acc1[zz].astype(f32) + rz1[way, zz].astype(f32)).astype(bf16)
        landed(rz0.at[way, zz], rz0_sems.at[way, zz])
        acc0[zz] = (acc0[zz].astype(f32) + rz0[way, zz].astype(f32)).astype(bf16)

    def chain(zz):
        landed(ry1.at[zz], ry1_sems.at[zz])
        acc1[zz] = (acc1[zz].astype(f32) + ry1[zz].astype(f32)).astype(bf16)
        for way, going, has, peer in ((0, z < zz, z > 0, up), (1, z > zz, z < last, down)):
            pl.when(both(going, has))(lambda: add_chain(way, zz))
            out.send(
                going,
                remote(
                    lambda zz=zz: acc1.at[zz], lambda way=way, zz=zz: rz1.at[way, zz],
                    lambda way=way, zz=zz: rz1_sems.at[way, zz], peer,
                ),
            )
            out.send(
                going,
                remote(
                    lambda zz=zz: acc0.at[zz], lambda way=way, zz=zz: rz0.at[way, zz],
                    lambda way=way, zz=zz: rz0_sems.at[way, zz], peer,
                ),
            )
    fold(order[0])
    for k in range(depth):
        if k + 1 < depth:
            fold(order[k + 1])
        chain(order[k])
    pl.when(z > 0)(lambda: add_chain(0, z))
    pl.when(z < last)(lambda: add_chain(1, z))
    out.send(
        None,
        remote(lambda: acc0.at[z, 1 - y], lambda: ry0, lambda: ry0_sem, over),
    )
    out_ref[tail] = acc1[z]
    landed(ry0, ry0_sem)
    out_ref[head] = (acc0[z, y].astype(f32) + ry0[...].astype(f32)).astype(bf16)
    out.drain()


def scatter_rows(part, gate, devices, split):
    depth = devices // 4
    tok, wide = part.shape[1], part.shape[2] + gate.shape[2]
    rest = tok - split
    bf = lambda *shape: pltpu.VMEM(shape + (wide,), jnp.bfloat16)
    dma = pltpu.SemaphoreType.DMA
    return pl.pallas_call(
        lambda *refs: scatter_kernel(depth, split, *refs),
        out_shape=jax.ShapeDtypeStruct((tok, wide), part.dtype),
        in_specs=[pl.BlockSpec(memory_space=pltpu.VMEM)] * 2,
        out_specs=pl.BlockSpec(memory_space=pltpu.VMEM),
        scratch_shapes=[
            bf(depth, 2, tok), bf(depth, 2, split), bf(depth, rest), bf(depth, rest),
            bf(depth, rest), bf(2, depth, 2, split), bf(2, depth, rest), bf(split),
            dma((9 * depth + 2,)), dma((depth, 2, 2)), dma((depth,)), dma((2, depth)),
            dma((2, depth)), dma,
        ],
        compiler_params=pltpu.CompilerParams(
            collective_id=1, has_side_effects=True, vmem_limit_bytes=VMEM_GRANT
        ),
    )(part, gate)


def keep_plan(gates, row_ids, replica_table, source, devices, home_cap, rep_cap):
    tok = row_ids.shape[0]
    experts = jnp.arange(devices, dtype=jnp.int32)
    hot = row_ids[:, :, None] == experts[None, None, :]
    named = jnp.any(hot, axis=1)
    dense_gate = jnp.sum(jnp.where(hot, gates.astype(jnp.float32)[:, :, None], 0.0), axis=1)
    copies = 1 + jnp.sum((replica_table[:, None] == experts[None, :]).astype(jnp.int32), axis=0)
    order = jnp.arange(tok, dtype=jnp.int32)
    earlier = (order[:, None] > order[None, :]).astype(jnp.bfloat16)
    rank = jnp.dot(earlier, named.astype(jnp.bfloat16), preferred_element_type=jnp.float32)
    many = copies.astype(jnp.float32)[None, :]
    position = jnp.floor((rank + 0.5) / many)
    turn = rank + source.astype(jnp.float32)
    copy_index = turn - many * jnp.floor((turn + 0.5) / many)
    limit = jnp.where(copy_index < 0.5, float(home_cap), float(rep_cap))
    kept = named & (position < limit)
    return jnp.where(kept, dense_gate, 0.0).astype(jnp.bfloat16)


def row_grads(x, dy, gate, gate_w, up_w, down_w):
    a = jnp.dot(x, gate_w, preferred_element_type=jnp.float32)
    b = jnp.dot(x, up_w, preferred_element_type=jnp.float32)
    u = lax.dot_general(dy, down_w, contract_cols, preferred_element_type=jnp.float32)
    sig = jax.nn.sigmoid(a)
    act = a * sig
    product = act * b
    hidden = product.astype(jnp.bfloat16).astype(jnp.float32)
    gate_grad = jnp.sum(hidden * u, axis=1, keepdims=True)
    gate_grad = jnp.where(gate > 0, gate_grad, 0.0)
    hg = (gate * product).astype(jnp.bfloat16)
    gu = gate * u
    da = (gu * b * sig * (1.0 + a * (1.0 - sig))).astype(jnp.bfloat16)
    db = (gu * act).astype(jnp.bfloat16)
    dx = lax.dot_general(da, gate_w, contract_cols, preferred_element_type=jnp.float32)
    dx = dx + lax.dot_general(db, up_w, contract_cols, preferred_element_type=jnp.float32)
    return gate_grad, hg, da, db, dx


def weight_grads(x, dy, hg, da, db):
    dwg = lax.dot_general(x, da, contract_rows, preferred_element_type=jnp.float32)
    dwu = lax.dot_general(x, db, contract_rows, preferred_element_type=jnp.float32)
    dwd = lax.dot_general(hg, dy, contract_rows, preferred_element_type=jnp.float32)
    return dwg, dwu, dwd


def on_device(tokens_in, grad_out, gates, expert_ids, replica_table, w_gate, w_up, w_down):
    devices = lax.axis_size("expert")
    me = lax.axis_index("expert")
    tok, width = tokens_in.shape
    home_cap = max(2, 5 * tok * TOP // (4 * devices))
    rep_cap = max(2, tok * TOP // (2 * devices))
    kept_gate = keep_plan(gates, expert_ids, replica_table, me, devices, home_cap, rep_cap)
    lanes = -(-devices // 128) * 128
    kept_gate = jnp.pad(kept_gate, ((0, 0), (0, lanes - devices)))
    payload = jnp.concatenate([tokens_in, grad_out, kept_gate], axis=1)
    chunks = max(1, devices * tok // ROWS_PER_CHUNK)
    part = tok // chunks
    relayed = chunks == 1 and devices % 4 == 0 and tok % 32 == 0
    split = max(16, tok // 8 // 16 * 16)
    mine = jnp.arange(lanes, dtype=jnp.int32)[None, :] == me
    backs, sums = [], None
    for c in range(chunks):
        if relayed:
            rows, da, db, hg, dx, spread = gather_rows(
                payload, w_gate[0], w_up[0], w_down[0], devices, split
            )
            backs.append(scatter_rows(dx, spread, devices, split))
            rows, da, db, hg = [v.reshape(devices * tok, -1) for v in (rows, da, db, hg)]
        else:
            rows = lax.all_gather(payload[c * part : (c + 1) * part], "expert", axis=0, tiled=True)
            gate = jnp.sum(
                jnp.where(mine, rows[:, 2 * width :].astype(jnp.float32), 0.0),
                axis=1,
                keepdims=True,
            )
            gate_grad, hg, da, db, dx = row_grads(
                rows[:, :width], rows[:, width : 2 * width], gate, w_gate[0], w_up[0], w_down[0]
            )
            spread = jnp.where(mine, gate_grad, 0.0).astype(jnp.bfloat16)
            back = jnp.concatenate([dx.astype(jnp.bfloat16), spread], axis=1)
            backs.append(lax.psum_scatter(back, "expert", scatter_dimension=0, tiled=True))
        grads = weight_grads(rows[:, :width], rows[:, width : 2 * width], hg, da, db)
        sums = grads if sums is None else [p + q for p, q in zip(sums, grads)]
        if c + 1 < chunks:
            payload, sums = lax.optimization_barrier((payload, sums))
    back = jnp.concatenate(backs, axis=0)
    experts = jnp.arange(devices, dtype=jnp.int32)
    hot = expert_ids[:, :, None] == experts[None, None, :]
    picked = jnp.where(hot, back[:, None, width : width + devices].astype(jnp.float32), 0.0)
    grad_gates = jnp.sum(picked, axis=2).astype(jnp.bfloat16)
    return (back[:, :width], grad_gates, *[g.astype(jnp.bfloat16)[None] for g in sums])


def solution(mesh):
    return jax.shard_map(
        on_device,
        mesh=mesh,
        in_specs=(
            P(("groups", "expert"), None),
            P(("groups", "expert"), None),
            P(("groups", "expert"), None),
            P(("groups", "expert"), None),
            P("groups"),
            P("expert", None, None),
            P("expert", None, None),
            P("expert", None, None),
        ),
        out_specs=(
            P(("groups", "expert"), None),
            P(("groups", "expert"), None),
            P(("groups", "expert"), None, None),
            P(("groups", "expert"), None, None),
            P(("groups", "expert"), None, None),
        ),
        check_vma=False,
    )
```
